32 devices in a mesh: win: 4 (over z), sec: 8 (over y, x, core).
Axes of the slice: x: 2, y: 2, z: 4, core: 2. Of those that a mesh axis runs over, the one named last changes fastest.
Arguments:
- initial: bfloat16 [5, 8, 24, 512], P(None, 'win'), may hold values from -6 to 6
- props: bfloat16 [8, 8, 2, 256, 256], P('sec'), may hold values from -0.25 to 0.25
- screen: float32 [8, 8, 256], P('sec', 'win'), may hold values from -3.140625 to 3.140625
- links: int32 [8, 8, 6], P('sec', 'win'), may hold values from 0 to 7, as said below
- kinds: int32 [8, 8, 6], P('sec', 'win'), may hold values from 0 to 7
- counts: int32 [8, 8], P('sec', 'win'), may hold values from 1 to 6
Outputs:
- fields: bfloat16 [8, 5, 8, 24, 512], P('sec', None, 'win')
The draws below stay inside these ranges and needn't reach their ends.
Inputs may be any that keep to these rules, and one draw needn't show every extreme that they name: links[s, w, l] lies within w - 1 to w + 1.
All inputs are finite; a program needn't handle non-finite values.
Results may differ from the reference program's by a relative error of at most 0.033.
Values may be sent and summed in bfloat16 or wider, within the bound.
A program may use at most 64 MiB of HBM per device.

```python
import jax
import jax.numpy as jnp
from jax import lax

K = 256
S = 24
F = 5
L = 6
NPROP = 8
W = 8
NSEC = 8


def draw_links(key, part):
    offsets = jax.random.randint(key, (NSEC, W, L), -1, 2)
    base = jnp.arange(W, dtype=jnp.int32)[None, :, None]
    return jnp.clip(base + offsets, 0, W - 1).astype(jnp.int32)


def with_ends(entries, key, least, largest):
    longest = entries.shape.index(max(entries.shape))
    spots = []
    for shift in (0, 1):
        where = [jax.random.randint(jax.random.fold_in(key, axis), (), 0, length) for axis, length in enumerate(entries.shape)]
        where[longest] = (where[longest] + shift) % entries.shape[longest]
        spots.append(tuple(where))
    return entries.at[spots[0]].set(least).at[spots[1]].set(largest)


def block_levels(rng, shape, pieces, low, high):
    level = 1.0
    for axis_at, blocks in pieces:
        steps = jax.random.uniform(jax.random.fold_in(jax.random.fold_in(rng, 6), axis_at), (blocks,), jnp.float32, low / len(pieces), high / len(pieces))
        level = level * jnp.repeat(jnp.exp(steps), shape[axis_at] // blocks).reshape((-1,) + (1,) * (len(shape) - 1 - axis_at))
    return level


def gaussian(own_key, shape, scale, limit, cuts=(), kind=jnp.bfloat16):
    entries = scale * jax.random.normal(own_key, shape, jnp.float32)
    if cuts:
        entries = entries * block_levels(own_key, shape, cuts, -0.22, 0.18)
    return jnp.clip(entries, -limit, limit).astype(kind)


def setup_inputs(seed: int = 0) -> dict:
    splits = jax.random.split(jax.random.key(seed), 7)
    return {
        "initial": gaussian(splits[0], (F, W, S, 2 * K), 1.0, 6.0, ((1, 4),)),
        "props": gaussian(splits[1], (NSEC, NPROP, 2, K, K), (2 * K) ** -0.5, 0.25, ((0, 8),)),
        "screen": jnp.clip(jax.random.uniform(splits[2], (NSEC, W, K), jnp.float32, -3.140625, 3.140625), -3.140625, 3.140625),
        "links": draw_links(jax.random.fold_in(splits[6], 71), 0),
        "kinds": with_ends(jax.random.randint(splits[4], (NSEC, W, L), 0, NPROP), jax.random.fold_in(splits[4], 1), 0, NPROP - 1).astype(jnp.int32),
        "counts": with_ends(jax.random.randint(splits[5], (NSEC, W), 1, L + 1), jax.random.fold_in(splits[5], 1), 1, L).astype(jnp.int32),
    }


def build_blocks(section_table):
    real_part = section_table[:, 0].astype(jnp.float32)
    imag_part = section_table[:, 1].astype(jnp.float32)
    upper = jnp.concatenate([real_part, imag_part], axis=-1)
    lower = jnp.concatenate([-imag_part, real_part], axis=-1)
    return jnp.concatenate([upper, lower], axis=-2)

def section_step(field, inputs):
    section_table, screen_phase, link_rows, kind_rows, count_rows = inputs
    blocks = build_blocks(section_table)
    field_wide = field.astype(jnp.float32)
    gathered = field_wide[:, link_rows]
    scaled = lax.rsqrt(count_rows.astype(jnp.float32))
    weighting = (jnp.arange(L)[None, :] < count_rows[:, None]).astype(jnp.float32) * scaled[:, None]
    total = jnp.zeros(field.shape, jnp.float32)
    for entry in range(NPROP):
        picked = weighting * (kind_rows == entry).astype(jnp.float32)
        mixed = jnp.einsum('wl,fwlsc->fwsc', picked, gathered, precision=lax.Precision.HIGHEST)
        total = total + jnp.einsum('fwsc,cd->fwsd', mixed, blocks[entry], precision=lax.Precision.HIGHEST)
    real_out = total[..., :K]
    imag_out = total[..., K:]
    cosine = jnp.cos(screen_phase)[None, :, None, :]
    sine_part = jnp.sin(screen_phase)[None, :, None, :]
    result = jnp.concatenate([real_out * cosine - imag_out * sine_part, real_out * sine_part + imag_out * cosine], axis=-1).astype(jnp.bfloat16)
    return (result, result)

def reference(initial, props, screen, links, kinds, counts):
    final_field, fields = lax.scan(section_step, initial, (props, screen, links, kinds, counts))
    return fields
```

```python
import functools

import jax
import jax.numpy as jnp
from jax import lax
from jax.experimental import pallas as pl
from jax.experimental.pallas import tpu as pltpu
from jax.sharding import PartitionSpec as P

MESH = pl.DeviceIdType.MESH
REACH = 2


def kernel(
    wins, secs, group, links, kinds, counts, screen, initial, props, out,
    inbox, stage, table, mixed, meta, table_sem, seed_sem, meta_sem, send_sem, recv_sem,
):
    z = lax.axis_index("win")
    s = lax.axis_index("sec")
    fronts, local, sources, width = initial.shape
    coeffs = width // 2
    entries = props.shape[0]
    length = links.shape[2]
    pieces = sources // group
    wide = local + 2
    even = lax.rem(s, 2) == 0
    odd = jnp.logical_not(even)
    has_low = z > 0
    has_high = z < wins - 1
    first = s == 0
    sends = s < secs - 1
    sides = has_low.astype(jnp.int32) + has_high.astype(jnp.int32)

    loads = [
        pltpu.make_async_copy(props.at[:, part], table.at[part], table_sem.at[part])
        for part in (0, 1)
    ]
    for load in loads:
        load.start()

    barrier = pltpu.get_barrier_semaphore()

    def greet(win, sec):
        pl.semaphore_signal(barrier, inc=1, device_id=(win, sec), device_id_type=MESH)

    def remote(source, target, send, receive, win, sec):
        return pltpu.make_async_remote_copy(
            src_ref=source, dst_ref=target, send_sem=send, recv_sem=receive,
            device_id=(win, sec), device_id_type=MESH,
        )

    def arrived(ref, sem):
        pltpu.make_async_copy(ref, ref, sem).wait()

    @pl.when(even & has_low)
    def _():
        greet(z - 1, s)

    @pl.when(even & has_high)
    def _():
        greet(z + 1, s)

    @pl.when(s > 0)
    def _():
        greet(z, s - 1)

    @pl.when(even & (s > 0) & has_low)
    def _():
        greet(z - 1, s - 1)

    @pl.when(even & (s > 0) & has_high)
    def _():
        greet(z + 1, s - 1)

    def rows_of(g):
        return pl.ds(pl.multiple_of(g * group, group), group)

    @pl.when(first)
    def _():
        for f in range(fronts):
            for g in range(pieces):
                rows = pl.ds(g * group, group)
                pltpu.make_async_copy(
                    initial.at[f, :, rows], inbox.at[f, REACH : REACH + local, rows],
                    recv_sem.at[f * pieces + g],
                ).start()

    @pl.when(even & jnp.logical_not(has_low))
    def _():
        inbox[:, :REACH] = jnp.zeros((fronts, REACH, sources, width), jnp.bfloat16)
        meta[0] = jnp.zeros(meta.shape[1:], jnp.float32)

    @pl.when(even & jnp.logical_not(has_high))
    def _():
        inbox[:, REACH + local :] = jnp.zeros((fronts, REACH, sources, width), jnp.bfloat16)
        meta[local + 1] = jnp.zeros(meta.shape[1:], jnp.float32)

    expected = jnp.where(
        even, sides + sends.astype(jnp.int32), jnp.where(sends, 1 + sides, 0)
    )

    @pl.when(expected > 0)
    def _():
        pl.semaphore_wait(barrier, expected)

    low_seed = (slice(0, REACH), slice(REACH + local, 2 * REACH + local))
    high_seed = (slice(local - REACH, local), slice(0, REACH))

    def seed(f, g, low):
        mine, theirs = low_seed if low else high_seed
        rows = pl.ds(g * group, group)
        return remote(
            initial.at[f, mine, rows], inbox.at[f, theirs, rows], seed_sem,
            recv_sem.at[f * pieces + g], z - 1 if low else z + 1, s,
        )

    @pl.when(first & has_low)
    def _():
        for f in range(fronts):
            for g in range(pieces):
                seed(f, g, True).start()

    @pl.when(first & has_high)
    def _():
        for f in range(fronts):
            for g in range(pieces):
                seed(f, g, False).start()

    codes_at = lax.broadcasted_iota(jnp.int32, (3 * entries, coeffs), 0)
    for w in range(local):
        live = counts[0, w]
        hits = jnp.zeros((3 * entries, coeffs), jnp.float32)
        for l in range(length):
            offset = links[0, w, l] - (z * local + w - 1)
            code = jnp.where(l < live, kinds[0, w, l] * 3 + offset, -1)
            hits = hits + (codes_at == code).astype(jnp.float32)
        meta[w + 1, : 3 * entries] = hits
        scale = lax.rsqrt(jnp.full((1, coeffs), live, jnp.int32).astype(jnp.float32))
        phase = screen[0, pl.ds(w, 1), :]
        meta[w + 1, pl.ds(3 * entries, 1)] = jnp.cos(phase) * scale
        meta[w + 1, pl.ds(3 * entries + 1, 1)] = jnp.sin(phase) * scale

    meta_low = remote(meta.at[1], meta.at[local + 1], meta_sem.at[0], meta_sem.at[1], z - 1, s)
    meta_high = remote(meta.at[local], meta.at[0], meta_sem.at[0], meta_sem.at[1], z + 1, s)

    @pl.when(even & has_low)
    def _():
        meta_low.start()

    @pl.when(even & has_high)
    def _():
        meta_high.start()

    def by_sides(wait):
        for count in (0, 1, 2):
            @pl.when(sides == count)
            def _():
                wait(count)

    def wait_meta(at):
        def wait(count):
            if count:
                arrived(meta.at[:count], meta_sem.at[at])
        return wait

    @pl.when(even)
    def _():
        by_sides(wait_meta(1))

    for load in loads:
        load.wait()

    depth = entries * coeffs

    def section(f, rows, windows, slot):
        held = [inbox[f, j, rows, :].astype(jnp.float32) for j in range(windows + 2)]
        tall = 2 * windows * group
        for entry in range(entries):
            stack = []
            for w in range(windows):
                parts = []
                for half in (0, 1):
                    at = slice(half * coeffs, (half + 1) * coeffs)
                    total = None
                    for d in range(3):
                        term = meta[slot + w, pl.ds(3 * entry + d, 1), :] * held[w + d][:, at]
                        total = term if total is None else total + term
                    parts.append(total)
                stack += parts
            left = entry * coeffs
            mixed[:tall, left : left + coeffs] = jnp.concatenate(stack, 0).astype(jnp.bfloat16)
        lhs = mixed[:tall]
        by_real, by_imag = (
            jnp.dot(lhs, table[part].reshape(depth, coeffs), preferred_element_type=jnp.float32)
            for part in (0, 1)
        )
        results = []
        for w in range(windows):
            top = 2 * w * group
            mid, low = top + group, top + 2 * group
            a = by_real[top:mid] - by_imag[mid:low]
            b = by_real[mid:low] + by_imag[top:mid]
            c = meta[slot + w, pl.ds(3 * entries, 1), :]
            d = meta[slot + w, pl.ds(3 * entries + 1, 1), :]
            results.append(((a * c - b * d).astype(jnp.bfloat16), (a * d + b * c).astype(jnp.bfloat16)))
        return results

    def even_step(u, carry):
        f = u // pieces
        rows = rows_of(u % pieces)

        def wait(count):
            arrived(inbox.at[f, : local + REACH * count, rows], recv_sem.at[u])

        by_sides(wait)
        for w, (a, b) in enumerate(section(f, rows, wide, 0)):
            stage[f, w, rows, :coeffs] = a
            stage[f, w, rows, coeffs:] = b
            if 0 < w <= local:
                out[0, f, w - 1, rows, :coeffs] = a
                out[0, f, w - 1, rows, coeffs:] = b

        @pl.when(sends)
        def _():
            remote(
                stage.at[f, :, rows], inbox.at[f, :wide, rows], send_sem, recv_sem.at[u], z, s + 1
            ).start()

        return carry

    def odd_step(u, carry):
        f = u // pieces
        rows = rows_of(u % pieces)
        arrived(inbox.at[f, :wide, rows], recv_sem.at[u])
        for w, (a, b) in enumerate(section(f, rows, local, 1)):
            out[0, f, w, rows, :coeffs] = a
            out[0, f, w, rows, coeffs:] = b

        def send(mine, theirs, win):
            remote(
                out.at[0, f, mine, rows], inbox.at[f, theirs, rows], send_sem, recv_sem.at[u], win, s + 1
            ).start()

        @pl.when(sends & has_low)
        def _():
            send(*low_seed, z - 1)

        @pl.when(sends & has_high)
        def _():
            send(*high_seed, z + 1)

        @pl.when(sends)
        def _():
            send(slice(0, local), slice(REACH, REACH + local), z)

        return carry

    units = fronts * pieces

    @pl.when(even)
    def _():
        lax.fori_loop(0, units, even_step, 0)

        @pl.when(sends)
        def _():
            arrived(stage, send_sem)

        by_sides(wait_meta(0))

    @pl.when(odd)
    def _():
        lax.fori_loop(0, units, odd_step, 0)

        def wait(count):
            arrived(inbox.at[:, : local + REACH * count], send_sem)

        @pl.when(sends)
        def _():
            by_sides(wait)

    @pl.when(first)
    def _():
        def wait(count):
            if count:
                arrived(inbox.at[:, : REACH * count], seed_sem)

        by_sides(wait)


def solution(mesh):
    wins, secs = mesh.shape["win"], mesh.shape["sec"]

    def run(initial, props, screen, links, kinds, counts):
        fronts, local, sources, width = initial.shape
        coeffs = width // 2
        entries = props.shape[1]
        group = 8 if sources % 8 == 0 else sources
        smem = pl.BlockSpec(memory_space=pltpu.SMEM)
        vmem = pl.BlockSpec(memory_space=pltpu.VMEM)
        whole = pl.BlockSpec(memory_space=pl.ANY)
        lines = -(-(3 * entries + 2) // 8) * 8
        return pl.pallas_call(
            functools.partial(kernel, wins, secs, group),
            out_shape=pltpu.VMEM((1, fronts, local, sources, width), jnp.bfloat16),
            in_specs=[smem, smem, smem, vmem, whole, whole],
            out_specs=vmem,
            scratch_shapes=[
                pltpu.VMEM((fronts, local + 2 * REACH, sources, width), jnp.bfloat16),
                pltpu.VMEM((fronts, local + 2, sources, width), jnp.bfloat16),
                pltpu.VMEM((2, entries, coeffs, coeffs), jnp.bfloat16),
                pltpu.VMEM((2 * (local + 2) * group, entries * coeffs), jnp.bfloat16),
                pltpu.VMEM((local + 2, lines, coeffs), jnp.float32),
                pltpu.SemaphoreType.DMA((2,)),
                pltpu.SemaphoreType.DMA,
                pltpu.SemaphoreType.DMA((2,)),
                pltpu.SemaphoreType.DMA,
                pltpu.SemaphoreType.DMA((fronts * (sources // group),)),
            ],
            compiler_params=pltpu.CompilerParams(collective_id=0, has_side_effects=True),
            name="beamlets",
        )(links, kinds, counts, screen, initial, props[0])

    placed = (
        P(None, "win", None, None),
        P("sec", None, None, None, None),
        P("sec", "win", None),
        P("sec", "win", None),
        P("sec", "win", None),
        P("sec", "win"),
    )
    return jax.shard_map(
        run,
        mesh=mesh,
        in_specs=placed,
        out_specs=P("sec", None, "win", None, None),
        check_vma=False,
    )
```
